32 devices in a mesh: space: 8 (over z, core), tm: 4 (over y, x).
Axes of the slice: x: 2, y: 2, z: 4, core: 2. Of those that a mesh axis runs over, the one named last changes fastest.
Arguments:
- snapshots: bfloat16 [32768, 512], P('space', 'tm'), may hold values from -6 to 6
- stencil_starts: int32 [512], P('tm'), may hold values from 0 to 508, as said below
- stencil_widths: int32 [512], P('tm'), may hold values from 4 to 40, as said below
- stencil_coeffs: bfloat16 [512, 40], P('tm'), may hold values from -2 to 2
- panels: bfloat16 [512, 256], P('tm'), may hold values from -0.25 to 0.25
Outputs:
- gram: float32 [512, 512], P(('tm', 'space'))
- modes: bfloat16 [32768, 256], P(('space', 'tm'))
The draws below stay inside these ranges and needn't reach their ends.
Inputs may be any that keep to these rules, and one draw needn't show every extreme that they name: `stencil_starts`: uniform time u's stencil starts inside its own time block, snapshots from (u // 128) * 128 to that plus 128 - 1, and ends before snapshot 512. `stencil_widths`: some stencil has width 40 and some has width 4.
All inputs are finite; a program needn't handle non-finite values.
Results may differ from the reference program's by a relative error of at most 0.0049.
Values may be sent and summed in bfloat16 or wider, within the bound.
A program may use at most 64 MiB of HBM per device.

```python
import jax
import jax.numpy as jnp
from jax import lax

U_DEV = 128
WMAX = 40
NMODE = 256
NU = 512
ROWS = 32768


def stencil_pair(key):
    blocks = NU // U_DEV
    block_high = jax.random.randint(jax.random.fold_in(key, 11), (blocks,), 8, WMAX + 1)
    high = jnp.repeat(block_high, U_DEV)
    raw = jax.random.randint(jax.random.fold_in(key, 12), (NU,), 0, 1048576)
    widths = 4 + raw % (high - 3)
    widths = widths.at[0].set(WMAX).at[1].set(4)
    offsets = jax.random.randint(jax.random.fold_in(key, 13), (NU,), 0, U_DEV)
    starts = jnp.arange(NU, dtype=jnp.int32) // U_DEV * U_DEV + offsets
    starts = jnp.minimum(starts, NU - widths)
    return (starts.astype(jnp.int32), widths.astype(jnp.int32))


def draw_stencil_starts(key, part):
    return stencil_pair(key)[0]


def draw_stencil_widths(key, part):
    return stencil_pair(key)[1]


def strengthened(drawn, key, source, target, shards_of, factor):
    def block_of(dim):
        return (jnp.arange(drawn.shape[dim]) // (drawn.shape[dim] // shards_of)).reshape((-1,) + (1,) * (drawn.ndim - 1 - dim))

    near = jax.random.permutation(key, shards_of)[block_of(target)]
    other_side = (block_of(target) + shards_of // 2) % shards_of
    return jnp.where((block_of(source) == near) | (block_of(source) == other_side), factor * drawn, drawn)


def block_scale(stream_key, dims, shards, low, largest):
    gain, own = 1.0, jax.random.fold_in(stream_key, 6)
    for axis_at, shards_of in shards:
        heights = jnp.exp(jax.random.uniform(jax.random.fold_in(own, axis_at), (shards_of,), jnp.float32, low / len(shards), largest / len(shards)))
        gain = gain * jnp.repeat(heights, dims[axis_at] // shards_of).reshape([-1 if axis == axis_at else 1 for axis in range(len(dims))])
    return gain


def bell_draw(own_key, dims, width, limit, pieces=(), kind=jnp.bfloat16):
    drawn = width * jax.random.normal(own_key, dims, jnp.float32)
    if pieces:
        drawn = drawn * block_scale(own_key, dims, pieces, -0.22, 0.18)
    return jnp.clip(drawn, -limit, limit).astype(kind)


def bell_draw_with(own_key, extent, spread, most, shards, heavy, held_as=jnp.bfloat16):
    result = spread * jax.random.normal(own_key, extent, jnp.float32)
    if shards:
        result = result * block_scale(own_key, extent, shards, -0.22, 0.18)
    return jnp.clip(strengthened(result, jax.random.fold_in(own_key, 3), *heavy), -most, most).astype(held_as)


def setup_inputs(seed: int = 0) -> dict:
    keys = jax.random.split(jax.random.key(seed), 6)
    return {
        "snapshots": bell_draw_with(keys[0], (ROWS, NU), 1.0, 6.0, ((0, 8), (1, 4)), (0, 1, 8, 2.0)),
        "stencil_starts": draw_stencil_starts(jax.random.fold_in(keys[5], 71), 0),
        "stencil_widths": draw_stencil_widths(jax.random.fold_in(keys[5], 71), 0),
        "stencil_coeffs": bell_draw(keys[3], (NU, WMAX), 0.3, 2.0, ((0, 4),)),
        "panels": bell_draw(keys[4], (NU, NMODE), NU ** -0.5, 0.25, ((0, 4),)),
    }


def stencil_matrix(stencil_starts, stencil_widths, stencil_coeffs):
    position = jnp.arange(NU, dtype=jnp.int32)[:, None]
    offset = position - stencil_starts[None, :]
    weights = jnp.zeros((NU, NU), jnp.float32)
    for step in range(WMAX):
        picked = (offset == step) & (step < stencil_widths[None, :])
        weights = weights + jnp.where(picked, stencil_coeffs[:, step].astype(jnp.float32)[None, :], 0.0)
    return weights.astype(jnp.bfloat16)


def reference(snapshots, stencil_starts, stencil_widths, stencil_coeffs, panels):
    weights = stencil_matrix(stencil_starts, stencil_widths, stencil_coeffs)
    resampled = jnp.dot(snapshots, weights, preferred_element_type=jnp.float32).astype(jnp.bfloat16)
    gram = lax.dot_general(resampled, resampled, (((0,), (0,)), ((), ())), preferred_element_type=jnp.float32)
    gram = gram * (1.0 / ROWS)
    modes = jnp.dot(resampled, panels, preferred_element_type=jnp.float32).astype(jnp.bfloat16)
    return gram, modes
```

```python
import functools

import jax
import jax.numpy as jnp
from jax import lax
from jax.experimental import pallas as pl
from jax.experimental.pallas import tpu as pltpu
from jax.sharding import PartitionSpec as P

F32 = jnp.float32
BF16 = jnp.bfloat16
CORES = 2
CHUNKS = 8


def shifted(value, axis, steps):
    count = lax.axis_size(axis)
    initial, last = (max(0, -steps), min(count, count - steps))
    return lax.ppermute(value, axis, [(source, source + steps) for source in range(initial, last)])


def on_device(snapshots, stencil_starts, stencil_widths, stencil_coeffs, panels):
    rows, block = snapshots.shape
    width_max = stencil_coeffs.shape[1]
    rim = shifted(snapshots[:, : width_max - 1], "tm", -1)
    extended = jnp.concatenate([snapshots, rim], axis=1)
    offsets = stencil_starts - lax.axis_index("tm") * block
    position = jnp.arange(block + width_max - 1, dtype=jnp.int32)[:, None]
    relative = position - offsets[None, :]
    steps = jnp.arange(width_max, dtype=jnp.int32)[:, None, None]
    picked = (relative[None, :, :] == steps) & (steps < stencil_widths[None, None, :])
    coeff_table = stencil_coeffs.T[:, None, :].astype(F32)
    weights = jnp.sum(jnp.where(picked, coeff_table, 0.0), axis=0).astype(BF16)
    resampled = jnp.dot(extended, weights, preferred_element_type=F32).astype(BF16)
    scale = 1.0 / (rows * lax.axis_size("space"))
    share = rows // lax.axis_size("tm")
    whole = lax.all_gather(resampled, "tm", axis=1, tiled=True)
    partial_value = lax.dot_general(
        resampled, whole, (((0,), (0,)), ((), ())), preferred_element_type=F32
    )
    every_panel = lax.all_gather(panels, "tm", axis=0, tiled=True)
    mine = lax.dynamic_slice_in_dim(whole, lax.axis_index("tm") * share, share, 0)
    modes = jnp.dot(mine, every_panel, preferred_element_type=F32).astype(BF16)
    partial_value = partial_value * scale
    gram = lax.psum_scatter(partial_value, "space", scatter_dimension=0, tiled=True)
    return (gram, modes)


def spread(packed, width_max, block):
    table = packed.astype(F32)
    rows = table.shape[0]
    moved = table[width_max : width_max + 1, :].astype(jnp.int32)
    index = lax.broadcasted_iota(jnp.int32, table.shape, 0)
    value = jnp.where(index < width_max, table, 0.0)
    step = 1
    while step < block:
        chosen = (moved & step) != 0
        if step < 8:
            other = pltpu.roll(value, step, 0)
        else:
            empty = jnp.zeros((step, block), F32)
            other = jnp.concatenate([empty, value], axis=0)
            value = jnp.concatenate([value, empty], axis=0)
        value = jnp.where(jnp.broadcast_to(chosen, value.shape), other, value)
        step *= 2
    return value


def kernel(
    nsp, ntm, chunks, halves, width_max,
    snap, starts_in, widths_in, coeffs_in, panels,
    gram_out, modes_out,
    starts, widths, coeffs,
    packed, weights, gathered, both, acc, tm_out, tm_in, z_out, z_in, panel_all,
    local_sem, table_send, table_recv, row_send, row_recv, pass_send, pass_recv,
    panel_send, panel_recv, relay_send, relay_recv, tm_send, tm_recv, z_send, z_recv,
):
    space = lax.axis_index("space")
    t = lax.axis_index("tm")
    zz, core = space // CORES, space % CORES
    nz = nsp // CORES
    nzh = nz // CORES
    block = snap.shape[1]
    share = snap.shape[0] // ntm
    piece = share // chunks
    nu = block * ntm
    wide = nu // halves
    half = block // CORES
    mine = nu // CORES
    own = half // nz
    others = ntm - 1

    def at(space_id, tm_id):
        return dict(device_id=(space_id, tm_id), device_id_type=pl.DeviceIdType.MESH)

    tm_peers = [t ^ mask for mask in range(ntm - 1, 0, -1)]
    partner = zz * CORES + (1 - core)

    def panel_rows(tm_id, core_id):
        return pl.ds(pl.multiple_of(core_id * mine + tm_id * half, half), half)

    barrier = pltpu.get_barrier_semaphore()
    for step in range(1, nsp):
        pl.semaphore_signal(barrier, inc=1, **at(lax.rem(space + step, nsp), t))
    for peer in tm_peers:
        pl.semaphore_signal(barrier, inc=1, **at(space, peer))

    columns = pl.ds(pl.multiple_of(t * block, block), block)
    small = [
        pltpu.make_async_copy(source, target, local_sem.at[i])
        for i, (source, target) in enumerate(
            [(starts_in, starts), (widths_in, widths), (coeffs_in, coeffs)]
        )
    ]
    own_rows = pltpu.make_async_copy(
        snap.at[pl.ds(pl.multiple_of(t * share, share), share), :], gathered.at[:, columns], local_sem.at[3]
    )
    own_panels = [
        pltpu.make_async_copy(panels.at[pl.ds(c * half, half), :], panel_all.at[panel_rows(t, c), :], local_sem.at[4 + c])
        for c in range(CORES)
    ]
    for copy in small:
        copy.start()
    own_rows.start()
    for copy in own_panels:
        copy.start()

    def send(src, dst, send_sem, recv_sem, space_id, tm_id):
        pltpu.make_async_remote_copy(
            src_ref=src, dst_ref=dst, send_sem=send_sem, recv_sem=recv_sem, **at(space_id, tm_id)).start()

    def wait_bytes(ref, sem):
        pltpu.make_async_copy(ref, ref, sem).wait()

    def send_rows(c):
        for peer in tm_peers:
            send(
                snap.at[pl.ds(pl.multiple_of(peer * share + c * piece, piece), piece), :],
                gathered.at[pl.ds(c * piece, piece), columns],
                row_send.at[0], row_recv.at[c], space, peer)

    pl.semaphore_wait(barrier, nsp - 1 + others)

    send_rows(0)

    for copy in small:
        copy.wait()
    prow = packed.shape[1]
    turned = jnp.concatenate(
        [coeffs[...].astype(F32), jnp.zeros((prow - width_max, block), F32)], axis=0
    )
    index = lax.broadcasted_iota(jnp.int32, turned.shape, 0)
    offset = (starts[...] - t * block).astype(F32)
    table = jnp.where(index < jnp.broadcast_to(widths[...], turned.shape), turned, 0.0)
    table = jnp.where(index == width_max, jnp.broadcast_to(offset, turned.shape), table)
    packed[t] = table.astype(BF16)
    for peer in tm_peers:
        send(packed.at[t], packed.at[t], table_send.at[0], table_recv.at[0], space, peer)

    for c in range(1, chunks):
        send_rows(c)
    for peer in tm_peers:
        send(
            panels.at[pl.ds(pl.multiple_of(core * half, half), half), :], panel_all.at[panel_rows(t, core), :],
            panel_send.at[0], panel_recv.at[0], space, peer)

    weights[...] = jnp.zeros_like(weights)
    acc[...] = jnp.zeros_like(acc)

    wait_bytes(packed.at[pl.ds(0, others)], table_recv.at[0])
    span = CORES * block
    for j in range(nu // span):
        left = spread(packed[2 * j], width_max, block)
        right = spread(packed[2 * j + 1], width_max, block)
        height = -(-(left.shape[0] + block) // 16) * 16
        left = jnp.concatenate([left, jnp.zeros((height - left.shape[0], block), F32)], axis=0)
        fill = jnp.zeros((height - block - right.shape[0], block), F32)
        right = jnp.concatenate([jnp.zeros((block, block), F32), right, fill], axis=0)
        low = lax.broadcasted_iota(jnp.int32, left.shape, 1) < half
        first, second = jnp.where(low, left, pltpu.roll(right, half, 1)), jnp.where(low, pltpu.roll(left, half, 1), right)
        height = min(height, nu - j * span)
        at_rows = slice(j * span, j * span + height)
        weights[at_rows, j * span : j * span + block] = first[:height].astype(BF16)
        weights[at_rows, j * span + block : (j + 1) * span] = second[:height].astype(BF16)

    own_rows.wait()

    def resample(c):
        at_rows = pl.ds(pl.multiple_of(c * piece, piece), piece)
        wait_bytes(gathered.at[at_rows, pl.ds(0, others * block)], row_recv.at[c])
        for j in range(nu // span):
            first = j * span
            last = min(first + span + block, nu)
            part = jnp.dot(
                gathered[at_rows, first:last], weights[first:last, first : first + span],
                preferred_element_type=F32,
            ).astype(BF16)
            both[c, core, :, j * block : (j + 1) * block] = part[:, :block]
            both[c, core, :, mine + j * block : mine + (j + 1) * block] = part[:, block:]
        send(both.at[c, core], both.at[c, core], pass_send.at[0], pass_recv.at[c], partner, t)

    def product(c, part):
        left = both[c, :, :, pl.ds(pl.multiple_of(core * mine, mine), mine)].reshape(CORES * piece, mine)
        right = both[c, :, :, part].reshape(CORES * piece, -1)
        value = lax.dot_general(left, right, (((0,), (0,)), ((), ())), preferred_element_type=F32)
        return value.reshape(ntm, half, right.shape[1])

    def partner_rows(c):
        wait_bytes(both.at[c, 1 - core], pass_recv.at[c])

    resample(0)

    def chunk_step(c, carry):
        resample(c)
        partner_rows(c - 1)
        acc[...] += product(c - 1, slice(None))
        return carry

    lax.fori_loop(1, chunks, chunk_step, 0)
    parts = [slice(h * wide, (h + 1) * wide) for h in range(halves)]
    partner_rows(chunks - 1)
    for h, part in enumerate(parts):
        total = acc[:, :, part] + product(chunks - 1, part)
        acc[:, :, part] = total
        tm_out[:, :, part] = total.astype(BF16)
        for i, peer in enumerate(tm_peers):
            send(tm_out.at[peer, :, part], tm_in.at[i, :, part], tm_send.at[0], tm_recv.at[h], space, peer)

    wait_bytes(panel_all.at[pl.ds(0, others * half), :], panel_recv.at[0])
    for origin in tm_peers:
        send(
            panel_all.at[panel_rows(origin, core), :], panel_all.at[panel_rows(origin, core), :],
            relay_send.at[0], relay_recv.at[0], partner, t)

    for h, part in enumerate(parts):
        wait_bytes(tm_in.at[:, :, part], tm_recv.at[h])
        total = acc[pl.ds(t, 1), :, part].reshape(half, wide)
        for i in range(others):
            total = total + tm_in[i, :, part].astype(F32)
        z_out[:, :, :, part] = total.astype(BF16).reshape(nzh, CORES, own, wide)
        for dz in range(nzh):
            for cc in range(CORES):
                to_z = core * nzh + dz
                here = (to_z == zz) & (cc == core)
                src, dst = z_out.at[dz, cc, :, part], z_in.at[zz, :, part]

                @pl.when(here)
                def _():
                    pltpu.make_async_copy(src, dst, z_recv.at[h]).start()

                @pl.when(jnp.logical_not(here))
                def _():
                    send(src, dst, z_send.at[0], z_recv.at[h], to_z * CORES + cc, t)

    for copy in own_panels:
        copy.wait()
    wait_bytes(panel_all.at[pl.ds(0, others * half), :], relay_recv.at[0])

    def modes_step(c, carry):
        at_rows = pl.ds(pl.multiple_of(c * piece, piece), piece)
        modes_out[at_rows, :] = jnp.dot(both[c, core], panel_all[...], preferred_element_type=F32).astype(BF16)
        return carry

    lax.fori_loop(0, chunks, modes_step, 0)

    wait_bytes(snap.at[pl.ds(0, others * share), :], row_send.at[0])
    wait_bytes(packed.at[pl.ds(0, others)], table_send.at[0])
    wait_bytes(both.at[:, 0], pass_send.at[0])
    wait_bytes(panel_all.at[pl.ds(0, others * half), :], panel_send.at[0])
    wait_bytes(panel_all.at[pl.ds(0, others * half), :], relay_send.at[0])
    wait_bytes(tm_in, tm_send.at[0])

    sums = []
    for h, part in enumerate(parts):
        wait_bytes(z_in.at[:, :, part], z_recv.at[h])
        final = z_in[0, :, part].astype(F32)
        for i in range(1, nz):
            final = final + z_in[i, :, part].astype(F32)
        sums.append(final * (1.0 / (snap.shape[0] * nsp)))
    final = jnp.concatenate(sums, axis=1)
    low = lax.broadcasted_iota(jnp.int32, (own, block), 1) < half
    for tile in range(ntm):
        at_tile = (tile // 2) * block
        left, right = final[:, at_tile : at_tile + block], final[:, mine + at_tile : mine + at_tile + block]
        if tile % 2:
            left = pltpu.roll(left, half, 1)
        else:
            right = pltpu.roll(right, half, 1)
        gram_out[:, tile * block : (tile + 1) * block] = jnp.where(low, left, right)

    inside = zz // nzh == core

    @pl.when(inside)
    def _():
        wait_bytes(z_in.at[pl.ds(0, nz - 1)], z_send.at[0])

    @pl.when(jnp.logical_not(inside))
    def _():
        wait_bytes(z_in, z_send.at[0])


def fused(nsp, ntm, snapshots, stencil_starts, stencil_widths, stencil_coeffs, panels):
    rows, block = snapshots.shape
    width_max = stencil_coeffs.shape[1]
    nmode = panels.shape[1]
    nu, share, nz = block * ntm, rows // ntm, nsp // CORES
    own, half = nu // (ntm * nsp), block // CORES
    chunks, halves = CHUNKS, 2
    piece = share // chunks
    prow = -(-(width_max + 1) // 16) * 16
    vmem = pl.BlockSpec(memory_space=pltpu.VMEM)
    hbm = pl.BlockSpec(memory_space=pltpu.HBM)
    dma = pltpu.SemaphoreType.DMA
    call = pl.pallas_call(
        functools.partial(kernel, nsp, ntm, chunks, halves, width_max),
        out_shape=(
            jax.ShapeDtypeStruct((own, nu), F32),
            jax.ShapeDtypeStruct((share, nmode), BF16),
        ),
        in_specs=[hbm, hbm, hbm, hbm, hbm],
        out_specs=(vmem, vmem),
        scratch_shapes=[
            pltpu.VMEM((1, block), jnp.int32),
            pltpu.VMEM((1, block), jnp.int32),
            pltpu.VMEM((width_max, block), BF16),
            pltpu.VMEM((ntm, prow, block), BF16),
            pltpu.VMEM((nu, nu), BF16),
            pltpu.VMEM((share, nu), BF16),
            pltpu.VMEM((chunks, CORES, piece, nu), BF16),
            pltpu.VMEM((ntm, half, nu), F32),
            pltpu.VMEM((ntm, half, nu), BF16),
            pltpu.VMEM((ntm - 1, half, nu), BF16),
            pltpu.VMEM((nz // CORES, CORES, own, nu), BF16),
            pltpu.VMEM((nz, own, nu), BF16),
            pltpu.VMEM((nu, nmode), BF16),
            dma((4 + CORES,)),
            dma((1,)),
            dma((1,)),
            dma((1,)),
            dma((chunks,)),
            dma((1,)),
            dma((chunks,)),
            dma((1,)),
            dma((1,)),
            dma((1,)),
            dma((1,)),
            dma((1,)),
            dma((halves,)),
            dma((1,)),
            dma((halves,)),
        ],
        compiler_params=pltpu.CompilerParams(
            collective_id=0, has_side_effects=True, vmem_limit_bytes=48 * 1024 * 1024
        ),
    )
    operands = (
        snapshots, stencil_starts.reshape(1, block), stencil_widths.reshape(1, block), stencil_coeffs.T, panels
    )
    values = call(*(pltpu.with_memory_space_constraint(operand, pltpu.HBM) for operand in operands))
    return pl.pallas_call(
        store,
        out_shape=tuple(jax.ShapeDtypeStruct(value.shape, value.dtype) for value in values),
        in_specs=[vmem, vmem],
        out_specs=(hbm, hbm),
        scratch_shapes=[dma((2,))],
    )(*(pltpu.with_memory_space_constraint(value, pltpu.VMEM) for value in values))


def store(gram, modes, gram_out, modes_out, sem):
    copies = [
        pltpu.make_async_copy(modes, modes_out, sem.at[0]),
        pltpu.make_async_copy(gram, gram_out, sem.at[1]),
    ]
    for copy in copies:
        copy.start()
    for copy in copies:
        copy.wait()


def solution(mesh):
    nsp, ntm = mesh.shape["space"], mesh.shape["tm"]

    def body(snapshots, stencil_starts, stencil_widths, stencil_coeffs, panels):
        rows, block = snapshots.shape
        own = block // nsp
        fits = block == 128 and own % 16 == 0 and nsp % (CORES * CORES) == 0 and ntm % 2 == 0 and ntm & (ntm - 1) == 0 and rows % (64 * ntm) == 0
        if fits and 4 * (block * ntm) ** 2 <= 4 * 1024 * 1024:
            return fused(nsp, ntm, snapshots, stencil_starts, stencil_widths, stencil_coeffs, panels)
        return on_device(snapshots, stencil_starts, stencil_widths, stencil_coeffs, panels)

    return jax.shard_map(
        body,
        mesh=mesh,
        in_specs=(P("space", "tm"), P("tm"), P("tm"), P("tm", None), P("tm", None)),
        out_specs=(P(("tm", "space"), None), P(("space", "tm"), None)),
        check_vma=False,
    )
```

```python
import functools

import jax
import jax.numpy as jnp
from jax import lax
from jax.experimental import pallas as pl
from jax.experimental.pallas import tpu as pltpu
from jax.sharding import PartitionSpec as P

F32 = jnp.float32
BF16 = jnp.bfloat16
CORES = 2
CHUNKS = 4
EARLY = 1


def shifted(value, axis, steps):
    count = lax.axis_size(axis)
    initial, last = (max(0, -steps), min(count, count - steps))
    return lax.ppermute(value, axis, [(source, source + steps) for source in range(initial, last)])


def on_device(snapshots, stencil_starts, stencil_widths, stencil_coeffs, panels):
    rows, block = snapshots.shape
    width_max = stencil_coeffs.shape[1]
    rim = shifted(snapshots[:, : width_max - 1], "tm", -1)
    extended = jnp.concatenate([snapshots, rim], axis=1)
    offsets = stencil_starts - lax.axis_index("tm") * block
    position = jnp.arange(block + width_max - 1, dtype=jnp.int32)[:, None]
    relative = position - offsets[None, :]
    steps = jnp.arange(width_max, dtype=jnp.int32)[:, None, None]
    picked = (relative[None, :, :] == steps) & (steps < stencil_widths[None, None, :])
    coeff_table = stencil_coeffs.T[:, None, :].astype(F32)
    weights = jnp.sum(jnp.where(picked, coeff_table, 0.0), axis=0).astype(BF16)
    resampled = jnp.dot(extended, weights, preferred_element_type=F32).astype(BF16)
    scale = 1.0 / (rows * lax.axis_size("space"))
    share = rows // lax.axis_size("tm")
    whole = lax.all_gather(resampled, "tm", axis=1, tiled=True)
    partial_value = lax.dot_general(
        resampled, whole, (((0,), (0,)), ((), ())), preferred_element_type=F32
    )
    every_panel = lax.all_gather(panels, "tm", axis=0, tiled=True)
    mine = lax.dynamic_slice_in_dim(whole, lax.axis_index("tm") * share, share, 0)
    modes = jnp.dot(mine, every_panel, preferred_element_type=F32).astype(BF16)
    partial_value = partial_value * scale
    gram = lax.psum_scatter(partial_value, "space", scatter_dimension=0, tiled=True)
    return (gram, modes)


def spread(packed, width_max, block):
    table = packed.astype(F32)
    rows = table.shape[0]
    moved = table[width_max : width_max + 1, :].astype(jnp.int32)
    index = lax.broadcasted_iota(jnp.int32, table.shape, 0)
    value = jnp.where(index < width_max, table, 0.0)
    step = 1
    while step < block:
        chosen = (moved & step) != 0
        if step < 8:
            other = pltpu.roll(value, step, 0)
        else:
            empty = jnp.zeros((step, block), F32)
            other = jnp.concatenate([empty, value], axis=0)
            value = jnp.concatenate([value, empty], axis=0)
        value = jnp.where(jnp.broadcast_to(chosen, value.shape), other, value)
        step *= 2
    return value


def kernel(
    nsp, ntm, chunks, width_max,
    snap, starts_in, widths_in, coeffs_in, panels,
    gram_out, modes_out,
    starts, widths, coeffs,
    packed, weights, gathered, both, acc, tm_out, tm_in, z_out, z_in,
    first_in, first_sum, first_out, second_in, panel_all,
    ready, local_sem, table_send, table_recv, row_send, row_recv, pass_send, pass_recv,
    panel_send, panel_recv, tm_send, tm_recv, z_send, z_recv, mix_send, mix_recv,
):
    space = lax.axis_index("space")
    t = lax.axis_index("tm")
    zz, core = space // CORES, space % CORES
    nz = nsp // CORES
    nzh = nz // CORES
    block = snap.shape[1]
    share = snap.shape[0] // ntm
    piece = share // chunks
    nu = block * ntm
    quarter = nu // 4
    half = block // CORES
    mine = nu // CORES
    own = half // nz
    others = ntm - 1

    def at(space_id, tm_id):
        return dict(device_id=(space_id, tm_id), device_id_type=pl.DeviceIdType.MESH)

    tm_peers = [t ^ mask for mask in range(ntm - 1, 0, -1)]
    partner = zz * CORES + (1 - core)

    near_peers = [peer for peer, mask in zip(tm_peers, range(ntm - 1, 0, -1)) if mask & (mask - 1) == 0]
    far_peers = [peer for peer, mask in zip(tm_peers, range(ntm - 1, 0, -1)) if mask & (mask - 1)]
    above, below = zz + 1 < nz, zz > 0

    barrier = pltpu.get_barrier_semaphore()
    for peer in near_peers:
        pl.semaphore_signal(barrier, inc=1, **at(space, peer))

    @pl.when(above)
    def _():
        pl.semaphore_signal(barrier, inc=1, **at(space + CORES, t))

    @pl.when(below)
    def _():
        pl.semaphore_signal(barrier, inc=1, **at(space - CORES, t))

    pl.semaphore_signal(barrier, inc=1, **at(partner, t))

    columns = pl.ds(pl.multiple_of(t * block, block), block)
    small = [
        pltpu.make_async_copy(source, target, local_sem.at[i])
        for i, (source, target) in enumerate(
            [(starts_in, starts), (widths_in, widths), (coeffs_in, coeffs)]
        )
    ]
    own_rows = pltpu.make_async_copy(
        snap.at[pl.ds(pl.multiple_of(t * share, share), share), :], gathered.at[:, columns], local_sem.at[3]
    )
    slot = pl.ds(pl.multiple_of(zz * own, own), own)
    panel_part = panels.at[pl.ds(pl.multiple_of(core * half + zz * own, own), own), :]
    own_panels = pltpu.make_async_copy(panel_part, panel_all.at[core, t, slot, :], local_sem.at[4])
    for copy in small:
        copy.start()
    own_rows.start()
    own_panels.start()

    def send(src, dst, send_sem, recv_sem, space_id, tm_id):
        pltpu.make_async_remote_copy(
            src_ref=src, dst_ref=dst, send_sem=send_sem, recv_sem=recv_sem, **at(space_id, tm_id)).start()

    def wait_bytes(ref, sem):
        pltpu.make_async_copy(ref, ref, sem).wait()

    def send_rows(c, peers):
        for peer in peers:
            send(
                snap.at[pl.ds(pl.multiple_of(peer * share + c * piece, piece), piece), :],
                gathered.at[pl.ds(c * piece, piece), columns],
                row_send.at[0], row_recv.at[c], space, peer)

    pl.semaphore_wait(barrier, len(near_peers) + 1 + above.astype(jnp.int32) + below.astype(jnp.int32))

    for peer in near_peers[-1:] if far_peers else []:
        pl.semaphore_signal(ready.at[0], inc=1, **at(space, peer))
    for copy in small:
        copy.wait()
    prow = packed.shape[1]
    turned = jnp.concatenate(
        [coeffs[...].astype(F32), jnp.zeros((prow - width_max, block), F32)], axis=0
    )
    index = lax.broadcasted_iota(jnp.int32, turned.shape, 0)
    offset = (starts[...] - t * block).astype(F32)
    table = jnp.where(index < jnp.broadcast_to(widths[...], turned.shape), turned, 0.0)
    table = jnp.where(index == width_max, jnp.broadcast_to(offset, turned.shape), table)
    packed[t] = table.astype(BF16)

    def send_table(peers):
        for peer in peers:
            send(packed.at[t], packed.at[t], table_send.at[0], table_recv.at[0], space, peer)

    send_table(near_peers)
    early = min(EARLY, chunks) if far_peers else 0
    for c in range(early):
        send_rows(c, near_peers)
    if far_peers:
        pl.semaphore_wait(ready.at[0], 1)
    send_table(far_peers)
    for c in range(early):
        send_rows(c, far_peers)
    for c in range(early, chunks):
        send_rows(c, tm_peers)
        if c == early:
            for peer in tm_peers:
                send(panel_part, panel_all.at[core, t, slot, :], panel_send.at[0], panel_recv.at[0], space, peer)

    weights[...] = jnp.zeros_like(weights)
    acc[...] = jnp.zeros_like(acc)

    line = ((1, zz, nz - 1 - zz, -CORES), (2, nz - 1 - zz, zz, CORES))

    def pass_on(sem, when, toward):
        @pl.when(when)
        def _():
            pl.semaphore_signal(ready.at[sem], inc=1, **at(space + toward, t))

    for sem, ahead, behind, toward in line:
        pass_on(sem, ahead > 0, toward)
    for step in range(1, nz):
        for sem, ahead, behind, toward in line:

            @pl.when(step <= behind)
            def _():
                pl.semaphore_wait(ready.at[sem], 1)

            pass_on(sem, (step <= behind) & (ahead > 0), toward)

    wait_bytes(packed.at[pl.ds(0, others)], table_recv.at[0])
    span = CORES * block
    for j in range(nu // span):
        left = spread(packed[2 * j], width_max, block)
        right = spread(packed[2 * j + 1], width_max, block)
        height = -(-(left.shape[0] + block) // 16) * 16
        left = jnp.concatenate([left, jnp.zeros((height - left.shape[0], block), F32)], axis=0)
        fill = jnp.zeros((height - block - right.shape[0], block), F32)
        right = jnp.concatenate([jnp.zeros((block, block), F32), right, fill], axis=0)
        low = lax.broadcasted_iota(jnp.int32, left.shape, 1) < half
        first, second = jnp.where(low, left, pltpu.roll(right, half, 1)), jnp.where(low, pltpu.roll(left, half, 1), right)
        height = min(height, nu - j * span)
        at_rows = slice(j * span, j * span + height)
        weights[at_rows, j * span : j * span + block] = first[:height].astype(BF16)
        weights[at_rows, j * span + block : (j + 1) * span] = second[:height].astype(BF16)

    own_rows.wait()

    def resample(c):
        at_rows = pl.ds(pl.multiple_of(c * piece, piece), piece)
        wait_bytes(gathered.at[at_rows, pl.ds(0, others * block)], row_recv.at[c])
        for j in range(nu // span):
            first = j * span
            last = min(first + span + block, nu)
            part = jnp.dot(
                gathered[at_rows, first:last], weights[first:last, first : first + span],
                preferred_element_type=F32,
            ).astype(BF16)
            both[c, core, :, j * block : (j + 1) * block] = part[:, :block]
            both[c, core, :, mine + j * block : mine + (j + 1) * block] = part[:, block:]
        send(both.at[c, core], both.at[c, core], pass_send.at[0], pass_recv.at[c], partner, t)

    def product(c, part):
        left = both[c, :, :, pl.ds(pl.multiple_of(core * mine, mine), mine)].reshape(CORES * piece, mine)
        right = both[c, :, :, part].reshape(CORES * piece, -1)
        value = lax.dot_general(left, right, (((0,), (0,)), ((), ())), preferred_element_type=F32)
        return value.reshape(ntm, half, right.shape[1])

    def partner_rows(c):
        wait_bytes(both.at[c, 1 - core], pass_recv.at[c])

    lag = 1

    def resample_step(c, carry):
        resample(c)
        return carry

    def add_step(c, carry):
        partner_rows(c)
        acc[...] += product(c, slice(None))
        return carry

    def chunk_step(c, carry):
        resample(c)
        return add_step(c - lag, carry)

    lax.fori_loop(0, lag, resample_step, 0)

    own_panels.wait()
    wait_bytes(panel_all.at[core, pl.ds(0, others), slot], panel_recv.at[0])
    for d in range(1, nz):
        peer = lax.rem(zz + d, nz) * CORES + core
        send(panel_all.at[core, :, slot], panel_all.at[core, :, slot], panel_send.at[1], panel_recv.at[1], peer, t)
    lax.fori_loop(lag, chunks, chunk_step, 0)
    parts = [slice(nu - 2 * quarter, nu - quarter), slice(0, nu - 2 * quarter)]
    ahead_part = slice(nu - quarter, nu)
    partner_rows(chunks - 1)
    def finish(part):
        total = acc[:, :, part] + product(chunks - 1, part)
        acc[:, :, part] = total
        tm_out[:, :, part] = total.astype(BF16)

    def send_tm(h):
        for i, peer in enumerate(tm_peers):
            send(tm_out.at[peer, :, parts[h]], tm_in.at[i, :, parts[h]], tm_send.at[0], tm_recv.at[h], space, peer)

    def send_line(pick, target, send_sem, recv_sem):
        for dz in range(nzh):
            for cc in range(CORES):
                to_z = core * nzh + dz
                here = (to_z == zz) & (cc == core)
                source = pick(dz * CORES + cc)

                @pl.when(here)
                def _():
                    pltpu.make_async_copy(source, target, recv_sem).start()

                @pl.when(jnp.logical_not(here))
                def _():
                    send(source, target, send_sem, recv_sem, to_z * CORES + cc, t)

    finish(slice(nu - 2 * quarter, nu))
    send_line(
        lambda k: tm_out.at[:, pl.ds(k * own, own), ahead_part], first_in.at[zz], mix_send.at[0], mix_recv.at[0])
    send_tm(0)
    finish(parts[1])
    send_tm(1)

    for h, part in enumerate(parts):
        wait_bytes(tm_in.at[:, :, part], tm_recv.at[h])
        total = acc[pl.ds(t, 1), :, part].reshape(half, part.stop - part.start)
        for i in range(others):
            total = total + tm_in[i, :, part].astype(F32)
        z_out[:, :, part] = total.astype(BF16).reshape(nz, own, part.stop - part.start)
        send_line(lambda k: z_out.at[k, :, part], z_in.at[zz, :, part], z_send.at[0], z_recv.at[h])

    wait_bytes(panel_all.at[core, :, pl.ds(0, half - own)], panel_recv.at[1])
    send(panel_all.at[core], panel_all.at[core], panel_send.at[2], panel_recv.at[2], partner, t)
    wait_bytes(first_in, mix_recv.at[0])
    total = first_in[0].astype(F32)
    for i in range(1, nz):
        total = total + first_in[i].astype(F32)
    first_sum[...] = total
    first_out[...] = total.astype(BF16)
    for i, peer in enumerate(tm_peers):
        send(first_out.at[peer], second_in.at[i], mix_send.at[1], mix_recv.at[1], space, peer)
    wait_bytes(panel_all.at[1 - core], panel_recv.at[2])

    group = chunks // 2
    table = panel_all[...].reshape(nu, -1)
    for c in range(0, chunks, group):
        rows = both[c : c + group, core].reshape(group * piece, nu)
        value = jnp.dot(rows, table, preferred_element_type=F32)
        modes_out[c * piece : (c + group) * piece, :] = value.astype(BF16)

    wait_bytes(snap.at[pl.ds(0, others * share), :], row_send.at[0])
    wait_bytes(packed.at[pl.ds(0, others)], table_send.at[0])
    wait_bytes(both.at[:, 0], pass_send.at[0])
    wait_bytes(panel_all.at[core, pl.ds(0, others), slot], panel_send.at[0])
    wait_bytes(panel_all.at[core, :, pl.ds(0, half - own)], panel_send.at[1])
    wait_bytes(panel_all.at[core], panel_send.at[2])
    wait_bytes(tm_in, tm_send.at[0])

    wait_bytes(second_in, mix_send.at[1])

    wait_bytes(second_in, mix_recv.at[1])
    total = first_sum[pl.ds(t, 1)].reshape(own, quarter)
    for i in range(others):
        total = total + second_in[i].astype(F32)
    sums = [total]
    for h, part in enumerate(parts):
        wait_bytes(z_in.at[:, :, part], z_recv.at[h])
        total = z_in[0, :, part].astype(F32)
        for i in range(1, nz):
            total = total + z_in[i, :, part].astype(F32)
        sums.insert(0, total)
    final = jnp.concatenate(sums[:1] + sums[1:], axis=1) * (1.0 / (snap.shape[0] * nsp))
    low = lax.broadcasted_iota(jnp.int32, (own, block), 1) < half
    for tile in range(ntm):
        at_tile = (tile // 2) * block
        left, right = final[:, at_tile : at_tile + block], final[:, mine + at_tile : mine + at_tile + block]
        if tile % 2:
            left = pltpu.roll(left, half, 1)
        else:
            right = pltpu.roll(right, half, 1)
        gram_out[:, tile * block : (tile + 1) * block] = jnp.where(low, left, right)

    inside = zz // nzh == core

    @pl.when(inside)
    def _():
        wait_bytes(z_in.at[pl.ds(0, nz - 1)], z_send.at[0])
        wait_bytes(first_in.at[pl.ds(0, nz - 1)], mix_send.at[0])

    @pl.when(jnp.logical_not(inside))
    def _():
        wait_bytes(z_in, z_send.at[0])
        wait_bytes(first_in, mix_send.at[0])


def fused(nsp, ntm, snapshots, stencil_starts, stencil_widths, stencil_coeffs, panels):
    rows, block = snapshots.shape
    width_max = stencil_coeffs.shape[1]
    nmode = panels.shape[1]
    nu, share, nz = block * ntm, rows // ntm, nsp // CORES
    own, half = nu // (ntm * nsp), block // CORES
    chunks, quarter = CHUNKS, nu // 4
    piece = share // chunks
    prow = -(-(width_max + 1) // 16) * 16
    vmem = pl.BlockSpec(memory_space=pltpu.VMEM)
    hbm = pl.BlockSpec(memory_space=pltpu.HBM)
    dma = pltpu.SemaphoreType.DMA
    call = pl.pallas_call(
        functools.partial(kernel, nsp, ntm, chunks, width_max),
        out_shape=(
            jax.ShapeDtypeStruct((own, nu), F32),
            jax.ShapeDtypeStruct((share, nmode), BF16),
        ),
        in_specs=[hbm, hbm, hbm, hbm, hbm],
        out_specs=(vmem, vmem),
        scratch_shapes=[
            pltpu.VMEM((1, block), jnp.int32),
            pltpu.VMEM((1, block), jnp.int32),
            pltpu.VMEM((width_max, block), BF16),
            pltpu.VMEM((ntm, prow, block), BF16),
            pltpu.VMEM((nu, nu), BF16),
            pltpu.VMEM((share, nu), BF16),
            pltpu.VMEM((chunks, CORES, piece, nu), BF16),
            pltpu.VMEM((ntm, half, nu), F32),
            pltpu.VMEM((ntm, half, nu), BF16),
            pltpu.VMEM((ntm - 1, half, nu - quarter), BF16),
            pltpu.VMEM((nz, own, nu - quarter), BF16),
            pltpu.VMEM((nz, own, nu - quarter), BF16),
            pltpu.VMEM((nz, ntm, own, quarter), BF16),
            pltpu.VMEM((ntm, own, quarter), F32),
            pltpu.VMEM((ntm, own, quarter), BF16),
            pltpu.VMEM((ntm - 1, own, quarter), BF16),
            pltpu.VMEM((CORES, ntm, half, nmode), BF16),
            pltpu.SemaphoreType.REGULAR((3,)),
            dma((5,)),
            dma((1,)),
            dma((1,)),
            dma((1,)),
            dma((chunks,)),
            dma((1,)),
            dma((chunks,)),
            dma((3,)),
            dma((3,)),
            dma((1,)),
            dma((2,)),
            dma((1,)),
            dma((2,)),
            dma((2,)),
            dma((2,)),
        ],
        compiler_params=pltpu.CompilerParams(
            collective_id=0, has_side_effects=True, vmem_limit_bytes=48 * 1024 * 1024
        ),
    )
    operands = (
        snapshots, stencil_starts.reshape(1, block), stencil_widths.reshape(1, block), stencil_coeffs.T, panels
    )
    values = call(*(pltpu.with_memory_space_constraint(operand, pltpu.HBM) for operand in operands))
    return pl.pallas_call(
        store,
        out_shape=tuple(jax.ShapeDtypeStruct(value.shape, value.dtype) for value in values),
        in_specs=[vmem, vmem],
        out_specs=(hbm, hbm),
        scratch_shapes=[dma((2,))],
    )(*(pltpu.with_memory_space_constraint(value, pltpu.VMEM) for value in values))


def store(gram, modes, gram_out, modes_out, sem):
    copies = [
        pltpu.make_async_copy(modes, modes_out, sem.at[0]),
        pltpu.make_async_copy(gram, gram_out, sem.at[1]),
    ]
    for copy in copies:
        copy.start()
    for copy in copies:
        copy.wait()


def solution(mesh):
    nsp, ntm = mesh.shape["space"], mesh.shape["tm"]

    def body(snapshots, stencil_starts, stencil_widths, stencil_coeffs, panels):
        rows, block = snapshots.shape
        own = block // nsp
        fits = block == 128 and own % 16 == 0 and nsp % (CORES * CORES) == 0 and 2 <= ntm <= 4 and ntm & (ntm - 1) == 0 and rows % (64 * ntm) == 0 and block * ntm % 512 == 0
        if fits and 4 * (block * ntm) ** 2 <= 4 * 1024 * 1024:
            return fused(nsp, ntm, snapshots, stencil_starts, stencil_widths, stencil_coeffs, panels)
        return on_device(snapshots, stencil_starts, stencil_widths, stencil_coeffs, panels)

    return jax.shard_map(
        body,
        mesh=mesh,
        in_specs=(P("space", "tm"), P("tm"), P("tm"), P("tm", None), P("tm", None)),
        out_specs=(P(("tm", "space"), None), P(("space", "tm"), None)),
        check_vma=False,
    )
```

```python
import functools

import jax
import jax.numpy as jnp
from jax import lax
from jax.experimental import pallas as pl
from jax.experimental.pallas import tpu as pltpu
from jax.sharding import PartitionSpec as P

F32 = jnp.float32
BF16 = jnp.bfloat16
CORES = 2
SPLIT = (4, 4, 4, 4)


def shifted(value, axis, steps):
    count = lax.axis_size(axis)
    initial, last = (max(0, -steps), min(count, count - steps))
    return lax.ppermute(value, axis, [(source, source + steps) for source in range(initial, last)])


def on_device(snapshots, stencil_starts, stencil_widths, stencil_coeffs, panels):
    rows, block = snapshots.shape
    width_max = stencil_coeffs.shape[1]
    rim = shifted(snapshots[:, : width_max - 1], "tm", -1)
    extended = jnp.concatenate([snapshots, rim], axis=1)
    offsets = stencil_starts - lax.axis_index("tm") * block
    position = jnp.arange(block + width_max - 1, dtype=jnp.int32)[:, None]
    relative = position - offsets[None, :]
    steps = jnp.arange(width_max, dtype=jnp.int32)[:, None, None]
    picked = (relative[None, :, :] == steps) & (steps < stencil_widths[None, None, :])
    coeff_table = stencil_coeffs.T[:, None, :].astype(F32)
    weights = jnp.sum(jnp.where(picked, coeff_table, 0.0), axis=0).astype(BF16)
    resampled = jnp.dot(extended, weights, preferred_element_type=F32).astype(BF16)
    scale = 1.0 / (rows * lax.axis_size("space"))
    share = rows // lax.axis_size("tm")
    whole = lax.all_gather(resampled, "tm", axis=1, tiled=True)
    partial_value = lax.dot_general(
        resampled, whole, (((0,), (0,)), ((), ())), preferred_element_type=F32
    )
    every_panel = lax.all_gather(panels, "tm", axis=0, tiled=True)
    mine = lax.dynamic_slice_in_dim(whole, lax.axis_index("tm") * share, share, 0)
    modes = jnp.dot(mine, every_panel, preferred_element_type=F32).astype(BF16)
    partial_value = partial_value * scale
    gram = lax.psum_scatter(partial_value, "space", scatter_dimension=0, tiled=True)
    return (gram, modes)


def spread(packed, width_max, block):
    table = packed.astype(F32)
    rows = table.shape[0]
    moved = table[width_max : width_max + 1, :].astype(jnp.int32)
    index = lax.broadcasted_iota(jnp.int32, table.shape, 0)
    value = jnp.where(index < width_max, table, 0.0)
    step = 1
    while step < block:
        chosen = (moved & step) != 0
        if step < 8:
            other = pltpu.roll(value, step, 0)
        else:
            empty = jnp.zeros((step, block), F32)
            other = jnp.concatenate([empty, value], axis=0)
            value = jnp.concatenate([value, empty], axis=0)
        value = jnp.where(jnp.broadcast_to(chosen, value.shape), other, value)
        step *= 2
    return value


def kernel(
    nsp, ntm, width_max,
    snap, starts_in, widths_in, coeffs_in, panels,
    gram_out, modes_out,
    starts, widths, coeffs,
    packed, weights, gathered, both, acc, tm_out, tm_in, z_out, z_in,
    first_in, first_sum, first_out, second_in, panel_all,
    ready, local_sem, table_send, table_recv, row_send, row_recv, pass_send, pass_recv,
    panel_send, panel_recv, tm_send, tm_recv, z_send, z_recv, mix_send, mix_recv,
):
    space = lax.axis_index("space")
    t = lax.axis_index("tm")
    zz, core = space // CORES, space % CORES
    nz = nsp // CORES
    nzh = nz // CORES
    block = snap.shape[1]
    share = snap.shape[0] // ntm
    chunks = len(SPLIT)
    sizes = [part * share // sum(SPLIT) for part in SPLIT]
    begins = [sum(sizes[:c]) for c in range(chunks)]
    nu = block * ntm
    quarter = nu // 4
    half = block // CORES
    mine = nu // CORES
    own = half // nz
    others = ntm - 1

    def at(space_id, tm_id):
        return dict(device_id=(space_id, tm_id), device_id_type=pl.DeviceIdType.MESH)

    tm_peers = [t ^ mask for mask in range(ntm - 1, 0, -1)]
    partner = zz * CORES + (1 - core)

    near_peers = [peer for peer, mask in zip(tm_peers, range(ntm - 1, 0, -1)) if mask & (mask - 1) == 0]
    far_peers = [peer for peer, mask in zip(tm_peers, range(ntm - 1, 0, -1)) if mask & (mask - 1)]
    above, below = zz + 1 < nz, zz > 0

    barrier = pltpu.get_barrier_semaphore()
    for peer in near_peers:
        pl.semaphore_signal(barrier, inc=1, **at(space, peer))

    @pl.when(above)
    def _():
        pl.semaphore_signal(barrier, inc=1, **at(space + CORES, t))

    @pl.when(below)
    def _():
        pl.semaphore_signal(barrier, inc=1, **at(space - CORES, t))

    pl.semaphore_signal(barrier, inc=1, **at(partner, t))

    columns = pl.ds(pl.multiple_of(t * block, block), block)
    small = [
        pltpu.make_async_copy(source, target, local_sem.at[i])
        for i, (source, target) in enumerate(
            [(starts_in, starts), (widths_in, widths), (coeffs_in, coeffs)]
        )
    ]
    own_rows = pltpu.make_async_copy(
        snap.at[pl.ds(pl.multiple_of(t * share, share), share), :], gathered.at[:, columns], local_sem.at[3]
    )
    slot = pl.ds(pl.multiple_of(zz * own, own), own)
    panel_part = panels.at[pl.ds(pl.multiple_of(core * half + zz * own, own), own), :]
    own_panels = pltpu.make_async_copy(panel_part, panel_all.at[core, t, slot, :], local_sem.at[4])
    for copy in small:
        copy.start()
    own_rows.start()
    own_panels.start()

    def send(src, dst, send_sem, recv_sem, space_id, tm_id):
        pltpu.make_async_remote_copy(
            src_ref=src, dst_ref=dst, send_sem=send_sem, recv_sem=recv_sem, **at(space_id, tm_id)).start()

    def wait_bytes(ref, sem):
        pltpu.make_async_copy(ref, ref, sem).wait()

    def send_rows(c, peers):
        for peer in peers:
            send(
                snap.at[pl.ds(pl.multiple_of(peer * share + begins[c], 16), sizes[c]), :],
                gathered.at[pl.ds(begins[c], sizes[c]), columns],
                row_send.at[0], row_recv.at[c], space, peer)

    pl.semaphore_wait(barrier, len(near_peers) + 1 + above.astype(jnp.int32) + below.astype(jnp.int32))

    for peer in near_peers[-1:] if far_peers else []:
        pl.semaphore_signal(ready.at[0], inc=1, **at(space, peer))
    for copy in small:
        copy.wait()
    prow = packed.shape[1]
    turned = jnp.concatenate(
        [coeffs[...].astype(F32), jnp.zeros((prow - width_max, block), F32)], axis=0
    )
    index = lax.broadcasted_iota(jnp.int32, turned.shape, 0)
    offset = (starts[...] - t * block).astype(F32)
    table = jnp.where(index < jnp.broadcast_to(widths[...], turned.shape), turned, 0.0)
    table = jnp.where(index == width_max, jnp.broadcast_to(offset, turned.shape), table)
    packed[t] = table.astype(BF16)

    def send_table(peers):
        for peer in peers:
            send(packed.at[t], packed.at[t], table_send.at[0], table_recv.at[0], space, peer)

    send_table(near_peers)
    early = 1 if far_peers else 0
    for c in range(early):
        send_rows(c, near_peers)
    if far_peers:
        pl.semaphore_wait(ready.at[0], 1)
    send_table(far_peers)
    for c in range(early):
        send_rows(c, far_peers)
    for c in range(early, chunks):
        if c == early:
            for peer in tm_peers:
                send(panel_part, panel_all.at[core, t, slot, :], panel_send.at[0], panel_recv.at[0], space, peer)
        send_rows(c, tm_peers)

    weights[...] = jnp.zeros_like(weights)
    acc[...] = jnp.zeros_like(acc)

    line = ((1, zz, nz - 1 - zz, -CORES), (2, nz - 1 - zz, zz, CORES))

    def pass_on(sem, when, toward):
        @pl.when(when)
        def _():
            pl.semaphore_signal(ready.at[sem], inc=1, **at(space + toward, t))

    for sem, ahead, behind, toward in line:
        pass_on(sem, ahead > 0, toward)
    for step in range(1, nz):
        for sem, ahead, behind, toward in line:

            @pl.when(step <= behind)
            def _():
                pl.semaphore_wait(ready.at[sem], 1)

            pass_on(sem, (step <= behind) & (ahead > 0), toward)

    wait_bytes(packed.at[pl.ds(0, others)], table_recv.at[0])
    span = CORES * block
    for j in range(nu // span):
        left = spread(packed[2 * j], width_max, block)
        right = spread(packed[2 * j + 1], width_max, block)
        height = -(-(left.shape[0] + block) // 16) * 16
        left = jnp.concatenate([left, jnp.zeros((height - left.shape[0], block), F32)], axis=0)
        fill = jnp.zeros((height - block - right.shape[0], block), F32)
        right = jnp.concatenate([jnp.zeros((block, block), F32), right, fill], axis=0)
        low = lax.broadcasted_iota(jnp.int32, left.shape, 1) < half
        first, second = jnp.where(low, left, pltpu.roll(right, half, 1)), jnp.where(low, pltpu.roll(left, half, 1), right)
        height = min(height, nu - j * span)
        at_rows = slice(j * span, j * span + height)
        weights[at_rows, j * span : j * span + block] = first[:height].astype(BF16)
        weights[at_rows, j * span + block : (j + 1) * span] = second[:height].astype(BF16)

    own_rows.wait()

    def rows_of(c, core_id):
        return pl.ds(pl.multiple_of(CORES * begins[c] + core_id * sizes[c], 16), sizes[c])

    def resample(c):
        at_rows = slice(begins[c], begins[c] + sizes[c])
        wait_bytes(gathered.at[at_rows, pl.ds(0, others * block)], row_recv.at[c])
        for j in range(nu // span):
            first = j * span
            last = min(first + span + block, nu)
            part = jnp.dot(
                gathered[at_rows, first:last], weights[first:last, first : first + span],
                preferred_element_type=F32,
            ).astype(BF16)
            both[rows_of(c, core), j * block : (j + 1) * block] = part[:, :block]
            both[rows_of(c, core), mine + j * block : mine + (j + 1) * block] = part[:, block:]
        for i in range(2):
            count = sizes[c] // 2
            shared = both.at[pl.ds(pl.multiple_of(CORES * begins[c] + core * sizes[c] + i * count, 16), count)]
            send(shared, shared, pass_send.at[0], pass_recv.at[c], partner, t)

    def product(c, part, source=None):
        first, count = CORES * begins[c], CORES * sizes[c]
        if source is not None:
            first, count = first + source * sizes[c], sizes[c]
        at_rows = slice(first, first + count)
        left = both[at_rows, pl.ds(pl.multiple_of(core * mine, mine), mine)]
        right = both[at_rows, part]
        value = lax.dot_general(left, right, (((0,), (0,)), ((), ())), preferred_element_type=F32)
        return value.reshape(ntm, half, right.shape[1])

    def partner_rows(c):
        wait_bytes(both.at[rows_of(c, 1 - core)], pass_recv.at[c])

    def add(c, source=None):
        acc[...] += product(c, slice(None), source)

    late = chunks - 1
    for c in range(late):
        resample(c)
        if c > 0:
            partner_rows(c - 1)
            add(c - 1)
        if c == 1:
            own_panels.wait()
            wait_bytes(panel_all.at[core, pl.ds(0, others), slot], panel_recv.at[0])
            for d in range(1, nz):
                peer = lax.rem(zz + d, nz) * CORES + core
                shared = panel_all.at[core, :, slot]
                send(shared, shared, panel_send.at[1], panel_recv.at[1], peer, t)


    @pl.when(core != 0)
    def _():
        resample(late)

    partner_rows(late - 1)
    add(late - 1)

    @pl.when(core == 0)
    def _():
        resample(late)
        partner_rows(late)

    add(late, 1)


    @pl.when(core != 0)
    def _():
        partner_rows(late)

    parts = [slice(nu - 2 * quarter, nu - quarter), slice(0, nu - 2 * quarter)]
    ahead_part = slice(nu - quarter, nu)
    def finish(part):
        total = acc[:, :, part] + product(late, part, 0)
        acc[:, :, part] = total
        tm_out[:, :, part] = total.astype(BF16)

    def send_tm(h):
        for i, peer in enumerate(tm_peers):
            send(tm_out.at[peer, :, parts[h]], tm_in.at[i, :, parts[h]], tm_send.at[0], tm_recv.at[h], space, peer)

    def send_line(pick, target, send_sem, recv_sem):
        for dz in range(nzh):
            for cc in range(CORES):
                to_z = core * nzh + dz
                here = (to_z == zz) & (cc == core)
                source = pick(dz * CORES + cc)

                @pl.when(here)
                def _():
                    pltpu.make_async_copy(source, target, recv_sem).start()

                @pl.when(jnp.logical_not(here))
                def _():
                    send(source, target, send_sem, recv_sem, to_z * CORES + cc, t)

    finish(slice(nu - 2 * quarter, nu))
    send_line(
        lambda k: tm_out.at[:, pl.ds(k * own, own), ahead_part], first_in.at[zz], mix_send.at[0], mix_recv.at[0])
    send_tm(0)
    finish(parts[1])
    send_tm(1)

    wait_bytes(panel_all.at[core, :, pl.ds(0, half - own)], panel_recv.at[1])
    send(panel_all.at[core], panel_all.at[core], panel_send.at[2], panel_recv.at[2], partner, t)
    for h, part in enumerate(parts):
        wait_bytes(tm_in.at[:, :, part], tm_recv.at[h])
        total = acc[pl.ds(t, 1), :, part].reshape(half, part.stop - part.start)
        for i in range(others):
            total = total + tm_in[i, :, part].astype(F32)
        z_out[:, :, part] = total.astype(BF16).reshape(nz, own, part.stop - part.start)
        send_line(lambda k: z_out.at[k, :, part], z_in.at[zz, :, part], z_send.at[0], z_recv.at[h])

    wait_bytes(first_in, mix_recv.at[0])
    total = first_in[0].astype(F32)
    for i in range(1, nz):
        total = total + first_in[i].astype(F32)
    first_sum[...] = total
    first_out[...] = total.astype(BF16)
    for i, peer in enumerate(tm_peers):
        send(first_out.at[peer], second_in.at[i], mix_send.at[1], mix_recv.at[1], space, peer)
    wait_bytes(panel_all.at[1 - core], panel_recv.at[2])

    table = panel_all[...].reshape(nu, -1)
    for c in range(chunks):
        value = jnp.dot(both[rows_of(c, core), :], table, preferred_element_type=F32)
        modes_out[begins[c] : begins[c] + sizes[c], :] = value.astype(BF16)

    wait_bytes(snap.at[pl.ds(0, others * share), :], row_send.at[0])
    wait_bytes(packed.at[pl.ds(0, others)], table_send.at[0])
    wait_bytes(both.at[pl.ds(0, share)], pass_send.at[0])
    wait_bytes(panel_all.at[core, pl.ds(0, others), slot], panel_send.at[0])
    wait_bytes(panel_all.at[core, :, pl.ds(0, half - own)], panel_send.at[1])
    wait_bytes(panel_all.at[core], panel_send.at[2])
    wait_bytes(tm_in, tm_send.at[0])

    wait_bytes(second_in, mix_send.at[1])

    wait_bytes(second_in, mix_recv.at[1])
    total = first_sum[pl.ds(t, 1)].reshape(own, quarter)
    for i in range(others):
        total = total + second_in[i].astype(F32)
    sums = [total]
    for h, part in enumerate(parts):
        wait_bytes(z_in.at[:, :, part], z_recv.at[h])
        total = z_in[0, :, part].astype(F32)
        for i in range(1, nz):
            total = total + z_in[i, :, part].astype(F32)
        sums.insert(0, total)
    final = jnp.concatenate(sums[:1] + sums[1:], axis=1) * (1.0 / (snap.shape[0] * nsp))
    low = lax.broadcasted_iota(jnp.int32, (own, block), 1) < half
    for tile in range(ntm):
        at_tile = (tile // 2) * block
        left, right = final[:, at_tile : at_tile + block], final[:, mine + at_tile : mine + at_tile + block]
        if tile % 2:
            left = pltpu.roll(left, half, 1)
        else:
            right = pltpu.roll(right, half, 1)
        gram_out[:, tile * block : (tile + 1) * block] = jnp.where(low, left, right)

    inside = zz // nzh == core

    @pl.when(inside)
    def _():
        wait_bytes(z_in.at[pl.ds(0, nz - 1)], z_send.at[0])
        wait_bytes(first_in.at[pl.ds(0, nz - 1)], mix_send.at[0])

    @pl.when(jnp.logical_not(inside))
    def _():
        wait_bytes(z_in, z_send.at[0])
        wait_bytes(first_in, mix_send.at[0])


def fused(nsp, ntm, snapshots, stencil_starts, stencil_widths, stencil_coeffs, panels):
    rows, block = snapshots.shape
    width_max = stencil_coeffs.shape[1]
    nmode = panels.shape[1]
    nu, share, nz = block * ntm, rows // ntm, nsp // CORES
    own, half = nu // (ntm * nsp), block // CORES
    chunks, quarter = len(SPLIT), nu // 4
    prow = -(-(width_max + 1) // 16) * 16
    vmem = pl.BlockSpec(memory_space=pltpu.VMEM)
    hbm = pl.BlockSpec(memory_space=pltpu.HBM)
    dma = pltpu.SemaphoreType.DMA
    call = pl.pallas_call(
        functools.partial(kernel, nsp, ntm, width_max),
        out_shape=(
            jax.ShapeDtypeStruct((own, nu), F32),
            jax.ShapeDtypeStruct((share, nmode), BF16),
        ),
        in_specs=[hbm, hbm, hbm, hbm, hbm],
        out_specs=(vmem, vmem),
        scratch_shapes=[
            pltpu.VMEM((1, block), jnp.int32),
            pltpu.VMEM((1, block), jnp.int32),
            pltpu.VMEM((width_max, block), BF16),
            pltpu.VMEM((ntm, prow, block), BF16),
            pltpu.VMEM((nu, nu), BF16),
            pltpu.VMEM((share, nu), BF16),
            pltpu.VMEM((CORES * share, nu), BF16),
            pltpu.VMEM((ntm, half, nu), F32),
            pltpu.VMEM((ntm, half, nu), BF16),
            pltpu.VMEM((ntm - 1, half, nu - quarter), BF16),
            pltpu.VMEM((nz, own, nu - quarter), BF16),
            pltpu.VMEM((nz, own, nu - quarter), BF16),
            pltpu.VMEM((nz, ntm, own, quarter), BF16),
            pltpu.VMEM((ntm, own, quarter), F32),
            pltpu.VMEM((ntm, own, quarter), BF16),
            pltpu.VMEM((ntm - 1, own, quarter), BF16),
            pltpu.VMEM((CORES, ntm, half, nmode), BF16),
            pltpu.SemaphoreType.REGULAR((3,)),
            dma((5,)),
            dma((1,)),
            dma((1,)),
            dma((1,)),
            dma((chunks,)),
            dma((1,)),
            dma((chunks,)),
            dma((3,)),
            dma((3,)),
            dma((1,)),
            dma((2,)),
            dma((1,)),
            dma((2,)),
            dma((2,)),
            dma((2,)),
        ],
        compiler_params=pltpu.CompilerParams(
            collective_id=0, has_side_effects=True, vmem_limit_bytes=48 * 1024 * 1024
        ),
    )
    operands = (
        snapshots, stencil_starts.reshape(1, block), stencil_widths.reshape(1, block), stencil_coeffs.T, panels
    )
    values = call(*(pltpu.with_memory_space_constraint(operand, pltpu.HBM) for operand in operands))
    return pl.pallas_call(
        store,
        out_shape=tuple(jax.ShapeDtypeStruct(value.shape, value.dtype) for value in values),
        in_specs=[vmem, vmem],
        out_specs=(hbm, hbm),
        scratch_shapes=[dma((2,))],
    )(*(pltpu.with_memory_space_constraint(value, pltpu.VMEM) for value in values))


def store(gram, modes, gram_out, modes_out, sem):
    copies = [
        pltpu.make_async_copy(modes, modes_out, sem.at[0]),
        pltpu.make_async_copy(gram, gram_out, sem.at[1]),
    ]
    for copy in copies:
        copy.start()
    for copy in copies:
        copy.wait()


def solution(mesh):
    nsp, ntm = mesh.shape["space"], mesh.shape["tm"]

    def body(snapshots, stencil_starts, stencil_widths, stencil_coeffs, panels):
        rows, block = snapshots.shape
        own = block // nsp
        fits = block == 128 and own % 16 == 0 and nsp % (CORES * CORES) == 0 and 2 <= ntm <= 4 and ntm & (ntm - 1) == 0 and rows % (256 * ntm) == 0 and block * ntm % 512 == 0
        if fits and 4 * (block * ntm) ** 2 <= 4 * 1024 * 1024:
            return fused(nsp, ntm, snapshots, stencil_starts, stencil_widths, stencil_coeffs, panels)
        return on_device(snapshots, stencil_starts, stencil_widths, stencil_coeffs, panels)

    return jax.shard_map(
        body,
        mesh=mesh,
        in_specs=(P("space", "tm"), P("tm"), P("tm"), P("tm", None), P("tm", None)),
        out_specs=(P(("tm", "space"), None), P(("space", "tm"), None)),
        check_vma=False,
    )
```

```python
import functools

import jax
import jax.numpy as jnp
from jax import lax
from jax.experimental import pallas as pl
from jax.experimental.pallas import tpu as pltpu
from jax.sharding import PartitionSpec as P

F32 = jnp.float32
BF16 = jnp.bfloat16
CORES = 2
SPLIT = (4, 4, 4, 4)


def shifted(value, axis, steps):
    count = lax.axis_size(axis)
    initial, last = (max(0, -steps), min(count, count - steps))
    return lax.ppermute(value, axis, [(source, source + steps) for source in range(initial, last)])


def on_device(snapshots, stencil_starts, stencil_widths, stencil_coeffs, panels):
    rows, block = snapshots.shape
    width_max = stencil_coeffs.shape[1]
    rim = shifted(snapshots[:, : width_max - 1], "tm", -1)
    extended = jnp.concatenate([snapshots, rim], axis=1)
    offsets = stencil_starts - lax.axis_index("tm") * block
    position = jnp.arange(block + width_max - 1, dtype=jnp.int32)[:, None]
    relative = position - offsets[None, :]
    steps = jnp.arange(width_max, dtype=jnp.int32)[:, None, None]
    picked = (relative[None, :, :] == steps) & (steps < stencil_widths[None, None, :])
    coeff_table = stencil_coeffs.T[:, None, :].astype(F32)
    weights = jnp.sum(jnp.where(picked, coeff_table, 0.0), axis=0).astype(BF16)
    resampled = jnp.dot(extended, weights, preferred_element_type=F32).astype(BF16)
    scale = 1.0 / (rows * lax.axis_size("space"))
    share = rows // lax.axis_size("tm")
    whole = lax.all_gather(resampled, "tm", axis=1, tiled=True)
    partial_value = lax.dot_general(
        resampled, whole, (((0,), (0,)), ((), ())), preferred_element_type=F32
    )
    every_panel = lax.all_gather(panels, "tm", axis=0, tiled=True)
    mine = lax.dynamic_slice_in_dim(whole, lax.axis_index("tm") * share, share, 0)
    modes = jnp.dot(mine, every_panel, preferred_element_type=F32).astype(BF16)
    partial_value = partial_value * scale
    gram = lax.psum_scatter(partial_value, "space", scatter_dimension=0, tiled=True)
    return (gram, modes)


def spread(packed, width_max, block):
    table = packed.astype(F32)
    rows = table.shape[0]
    moved = table[width_max : width_max + 1, :].astype(jnp.int32)
    index = lax.broadcasted_iota(jnp.int32, table.shape, 0)
    value = jnp.where(index < width_max, table, 0.0)
    step = 1
    while step < block:
        chosen = (moved & step) != 0
        if step < 8:
            other = pltpu.roll(value, step, 0)
        else:
            empty = jnp.zeros((step, block), F32)
            other = jnp.concatenate([empty, value], axis=0)
            value = jnp.concatenate([value, empty], axis=0)
        value = jnp.where(jnp.broadcast_to(chosen, value.shape), other, value)
        step *= 2
    return value


def kernel(
    nsp, ntm, width_max,
    snap, starts_in, widths_in, coeffs_in, panels,
    gram_out, modes_out,
    starts, widths, coeffs,
    packed, weights, gathered, both, acc, tm_out, tm_in, z_out, z_in,
    first_in, first_sum, first_out, second_in, panel_all,
    ready, local_sem, table_send, table_recv, row_send, row_recv, pass_send, pass_recv,
    panel_send, panel_recv, tm_send, tm_recv, z_send, z_recv, mix_send, mix_recv,
):
    space = lax.axis_index("space")
    t = lax.axis_index("tm")
    zz, core = space // CORES, space % CORES
    nz = nsp // CORES
    nzh = nz // CORES
    block = snap.shape[1]
    share = snap.shape[0] // ntm
    chunks = len(SPLIT)
    sizes = [part * share // sum(SPLIT) for part in SPLIT]
    begins = [sum(sizes[:c]) for c in range(chunks)]
    nu = block * ntm
    quarter = nu // 4
    half = block // CORES
    mine = nu // CORES
    own = half // nz
    others = ntm - 1

    def at(space_id, tm_id):
        return dict(device_id=(space_id, tm_id), device_id_type=pl.DeviceIdType.MESH)

    tm_peers = [t ^ mask for mask in range(ntm - 1, 0, -1)]
    partner = zz * CORES + (1 - core)

    near_peers = [peer for peer, mask in zip(tm_peers, range(ntm - 1, 0, -1)) if mask & (mask - 1) == 0]
    far_peers = [peer for peer, mask in zip(tm_peers, range(ntm - 1, 0, -1)) if mask & (mask - 1)]
    above, below = zz + 1 < nz, zz > 0

    barrier = pltpu.get_barrier_semaphore()
    for peer in near_peers:
        pl.semaphore_signal(barrier, inc=1, **at(space, peer))

    @pl.when(above)
    def _():
        pl.semaphore_signal(barrier, inc=1, **at(space + CORES, t))

    @pl.when(below)
    def _():
        pl.semaphore_signal(barrier, inc=1, **at(space - CORES, t))

    pl.semaphore_signal(barrier, inc=1, **at(partner, t))

    columns = pl.ds(pl.multiple_of(t * block, block), block)
    small = [
        pltpu.make_async_copy(source, target, local_sem.at[i])
        for i, (source, target) in enumerate(
            [(starts_in, starts), (widths_in, widths), (coeffs_in, coeffs)]
        )
    ]
    own_rows = pltpu.make_async_copy(
        snap.at[pl.ds(pl.multiple_of(t * share, share), share), :], gathered.at[:, columns], local_sem.at[3]
    )
    slot = pl.ds(pl.multiple_of(zz * own, own), own)
    panel_part = panels.at[pl.ds(pl.multiple_of(core * half + zz * own, own), own), :]
    own_panels = pltpu.make_async_copy(panel_part, panel_all.at[core, t, slot, :], local_sem.at[4])
    for copy in small:
        copy.start()
    own_rows.start()
    own_panels.start()

    def send(src, dst, send_sem, recv_sem, space_id, tm_id):
        pltpu.make_async_remote_copy(
            src_ref=src, dst_ref=dst, send_sem=send_sem, recv_sem=recv_sem, **at(space_id, tm_id)).start()

    def wait_bytes(ref, sem):
        pltpu.make_async_copy(ref, ref, sem).wait()

    def send_rows(c, peers):
        for peer in peers:
            send(
                snap.at[pl.ds(pl.multiple_of(peer * share + begins[c], 16), sizes[c]), :],
                gathered.at[pl.ds(begins[c], sizes[c]), columns],
                row_send.at[0], row_recv.at[c], space, peer)

    pl.semaphore_wait(barrier, len(near_peers) + 1 + above.astype(jnp.int32) + below.astype(jnp.int32))

    for peer in near_peers[-1:] if far_peers else []:
        pl.semaphore_signal(ready.at[0], inc=1, **at(space, peer))
    for copy in small:
        copy.wait()
    prow = packed.shape[1]
    turned = jnp.concatenate(
        [coeffs[...].astype(F32), jnp.zeros((prow - width_max, block), F32)], axis=0
    )
    index = lax.broadcasted_iota(jnp.int32, turned.shape, 0)
    offset = (starts[...] - t * block).astype(F32)
    table = jnp.where(index < jnp.broadcast_to(widths[...], turned.shape), turned, 0.0)
    table = jnp.where(index == width_max, jnp.broadcast_to(offset, turned.shape), table)
    packed[t] = table.astype(BF16)

    def send_table(peers):
        for peer in peers:
            send(packed.at[t], packed.at[t], table_send.at[0], table_recv.at[0], space, peer)

    send_table(near_peers)
    early = 1 if far_peers else 0
    for c in range(early):
        send_rows(c, near_peers)
    if far_peers:
        pl.semaphore_wait(ready.at[0], 1)
    send_table(far_peers)
    for c in range(early):
        send_rows(c, far_peers)
    for c in range(early, chunks):
        if c == early:
            for peer in tm_peers:
                send(panel_part, panel_all.at[core, t, slot, :], panel_send.at[0], panel_recv.at[0], space, peer)
        send_rows(c, tm_peers)

    weights[...] = jnp.zeros_like(weights)
    acc[...] = jnp.zeros_like(acc)

    line = ((1, zz, nz - 1 - zz, -CORES), (2, nz - 1 - zz, zz, CORES))

    def pass_on(sem, when, toward):
        @pl.when(when)
        def _():
            pl.semaphore_signal(ready.at[sem], inc=1, **at(space + toward, t))

    for sem, ahead, behind, toward in line:
        pass_on(sem, ahead > 0, toward)
    for step in range(1, nz):
        for sem, ahead, behind, toward in line:

            @pl.when(step <= behind)
            def _():
                pl.semaphore_wait(ready.at[sem], 1)

            pass_on(sem, (step <= behind) & (ahead > 0), toward)

    wait_bytes(packed.at[pl.ds(0, others)], table_recv.at[0])
    span = CORES * block
    for j in range(nu // span):
        left = spread(packed[2 * j], width_max, block)
        right = spread(packed[2 * j + 1], width_max, block)
        height = -(-(left.shape[0] + block) // 16) * 16
        left = jnp.concatenate([left, jnp.zeros((height - left.shape[0], block), F32)], axis=0)
        fill = jnp.zeros((height - block - right.shape[0], block), F32)
        right = jnp.concatenate([jnp.zeros((block, block), F32), right, fill], axis=0)
        low = lax.broadcasted_iota(jnp.int32, left.shape, 1) < half
        first, second = jnp.where(low, left, pltpu.roll(right, half, 1)), jnp.where(low, pltpu.roll(left, half, 1), right)
        height = min(height, nu - j * span)
        at_rows = slice(j * span, j * span + height)
        weights[at_rows, j * span : j * span + block] = first[:height].astype(BF16)
        weights[at_rows, j * span + block : (j + 1) * span] = second[:height].astype(BF16)

    own_rows.wait()

    def rows_of(c, core_id):
        return pl.ds(pl.multiple_of(CORES * begins[c] + core_id * sizes[c], 16), sizes[c])

    def resample(c):
        at_rows = slice(begins[c], begins[c] + sizes[c])
        wait_bytes(gathered.at[at_rows, pl.ds(0, others * block)], row_recv.at[c])
        for j in range(nu // span):
            first = j * span
            last = min(first + span + block, nu)
            part = jnp.dot(
                gathered[at_rows, first:last], weights[first:last, first : first + span],
                preferred_element_type=F32,
            ).astype(BF16)
            both[rows_of(c, core), j * block : (j + 1) * block] = part[:, :block]
            both[rows_of(c, core), mine + j * block : mine + (j + 1) * block] = part[:, block:]
        for i in range(2):
            count = sizes[c] // 2
            shared = both.at[pl.ds(pl.multiple_of(CORES * begins[c] + core * sizes[c] + i * count, 16), count)]
            send(shared, shared, pass_send.at[0], pass_recv.at[c], partner, t)

    def product(c, part, source=None):
        first, count = CORES * begins[c], CORES * sizes[c]
        if source is not None:
            first, count = first + source * sizes[c], sizes[c]
        at_rows = slice(first, first + count)
        left = both[at_rows, pl.ds(pl.multiple_of(core * mine, mine), mine)]
        right = both[at_rows, part]
        value = lax.dot_general(left, right, (((0,), (0,)), ((), ())), preferred_element_type=F32)
        return value.reshape(ntm, half, right.shape[1])

    def partner_rows(c):
        wait_bytes(both.at[rows_of(c, 1 - core)], pass_recv.at[c])

    def add(c, source=None):
        acc[...] += product(c, slice(None), source)

    late = chunks - 1
    for c in range(late):
        resample(c)
        if c > 0:
            partner_rows(c - 1)
            add(c - 1)
        if c == 1:
            own_panels.wait()
            wait_bytes(panel_all.at[core, pl.ds(0, others), slot], panel_recv.at[0])
            for d in range(1, nz):
                peer = lax.rem(zz + d, nz) * CORES + core
                shared = panel_all.at[core, :, slot]
                send(shared, shared, panel_send.at[1], panel_recv.at[1], peer, t)


    @pl.when(core != 0)
    def _():
        resample(late)

    partner_rows(late - 1)
    add(late - 1)

    @pl.when(core == 0)
    def _():
        resample(late)
        partner_rows(late)

    add(late, 1)


    @pl.when(core != 0)
    def _():
        partner_rows(late)

    parts = [slice(0, nu - 2 * quarter), slice(nu - 2 * quarter, nu - quarter)]
    ahead_part = slice(nu - quarter, nu)
    def finish(part):
        total = acc[:, :, part] + product(late, part, 0)
        acc[:, :, part] = total
        tm_out[:, :, part] = total.astype(BF16)

    def send_tm(h):
        for i, peer in enumerate(tm_peers):
            send(tm_out.at[peer, :, parts[h]], tm_in.at[i, :, parts[h]], tm_send.at[0], tm_recv.at[h], space, peer)

    def send_line(pick, target, send_sem, recv_sem):
        for dz in range(nzh):
            for cc in range(CORES):
                to_z = core * nzh + dz
                here = (to_z == zz) & (cc == core)
                source = pick(dz * CORES + cc)

                @pl.when(here)
                def _():
                    pltpu.make_async_copy(source, target, recv_sem).start()

                @pl.when(jnp.logical_not(here))
                def _():
                    send(source, target, send_sem, recv_sem, to_z * CORES + cc, t)

    finish(slice(0, nu - 2 * quarter))
    send_tm(0)
    finish(slice(nu - 2 * quarter, nu))
    send_line(
        lambda k: tm_out.at[:, pl.ds(k * own, own), ahead_part], first_in.at[zz], mix_send.at[0], mix_recv.at[0])
    send_tm(1)

    wait_bytes(panel_all.at[core, :, pl.ds(0, half - own)], panel_recv.at[1])
    send(panel_all.at[core], panel_all.at[core], panel_send.at[2], panel_recv.at[2], partner, t)
    for h, part in enumerate(parts):
        wait_bytes(tm_in.at[:, :, part], tm_recv.at[h])
        total = acc[pl.ds(t, 1), :, part].reshape(half, part.stop - part.start)
        for i in range(others):
            total = total + tm_in[i, :, part].astype(F32)
        z_out[:, :, part] = total.astype(BF16).reshape(nz, own, part.stop - part.start)
        send_line(lambda k: z_out.at[k, :, part], z_in.at[zz, :, part], z_send.at[0], z_recv.at[h])

    wait_bytes(first_in, mix_recv.at[0])
    total = first_in[0].astype(F32)
    for i in range(1, nz):
        total = total + first_in[i].astype(F32)
    first_sum[...] = total
    first_out[...] = total.astype(BF16)
    for i, peer in enumerate(tm_peers):
        send(first_out.at[peer], second_in.at[i], mix_send.at[1], mix_recv.at[1], space, peer)
    wait_bytes(panel_all.at[1 - core], panel_recv.at[2])

    table = panel_all[...].reshape(nu, -1)
    for c in range(chunks):
        value = jnp.dot(both[rows_of(c, core), :], table, preferred_element_type=F32)
        modes_out[begins[c] : begins[c] + sizes[c], :] = value.astype(BF16)

    wait_bytes(snap.at[pl.ds(0, others * share), :], row_send.at[0])
    wait_bytes(packed.at[pl.ds(0, others)], table_send.at[0])
    wait_bytes(both.at[pl.ds(0, share)], pass_send.at[0])
    wait_bytes(panel_all.at[core, pl.ds(0, others), slot], panel_send.at[0])
    wait_bytes(panel_all.at[core, :, pl.ds(0, half - own)], panel_send.at[1])
    wait_bytes(panel_all.at[core], panel_send.at[2])
    wait_bytes(tm_in, tm_send.at[0])

    wait_bytes(second_in, mix_send.at[1])

    wait_bytes(second_in, mix_recv.at[1])
    total = first_sum[pl.ds(t, 1)].reshape(own, quarter)
    for i in range(others):
        total = total + second_in[i].astype(F32)
    ahead = total
    sums = []
    for h, part in enumerate(parts):
        wait_bytes(z_in.at[:, :, part], z_recv.at[h])
        total = z_in[0, :, part].astype(F32)
        for i in range(1, nz):
            total = total + z_in[i, :, part].astype(F32)
        sums.append(total)
    final = jnp.concatenate(sums + [ahead], axis=1) * (1.0 / (snap.shape[0] * nsp))
    low = lax.broadcasted_iota(jnp.int32, (own, block), 1) < half
    for tile in range(ntm):
        at_tile = (tile // 2) * block
        left, right = final[:, at_tile : at_tile + block], final[:, mine + at_tile : mine + at_tile + block]
        if tile % 2:
            left = pltpu.roll(left, half, 1)
        else:
            right = pltpu.roll(right, half, 1)
        gram_out[:, tile * block : (tile + 1) * block] = jnp.where(low, left, right)

    inside = zz // nzh == core

    @pl.when(inside)
    def _():
        wait_bytes(z_in.at[pl.ds(0, nz - 1)], z_send.at[0])
        wait_bytes(first_in.at[pl.ds(0, nz - 1)], mix_send.at[0])

    @pl.when(jnp.logical_not(inside))
    def _():
        wait_bytes(z_in, z_send.at[0])
        wait_bytes(first_in, mix_send.at[0])


def fused(nsp, ntm, snapshots, stencil_starts, stencil_widths, stencil_coeffs, panels):
    rows, block = snapshots.shape
    width_max = stencil_coeffs.shape[1]
    nmode = panels.shape[1]
    nu, share, nz = block * ntm, rows // ntm, nsp // CORES
    own, half = nu // (ntm * nsp), block // CORES
    chunks, quarter = len(SPLIT), nu // 4
    prow = -(-(width_max + 1) // 16) * 16
    vmem = pl.BlockSpec(memory_space=pltpu.VMEM)
    hbm = pl.BlockSpec(memory_space=pltpu.HBM)
    dma = pltpu.SemaphoreType.DMA
    call = pl.pallas_call(
        functools.partial(kernel, nsp, ntm, width_max),
        out_shape=(
            jax.ShapeDtypeStruct((own, nu), F32),
            jax.ShapeDtypeStruct((share, nmode), BF16),
        ),
        in_specs=[hbm, hbm, hbm, hbm, hbm],
        out_specs=(vmem, vmem),
        scratch_shapes=[
            pltpu.VMEM((1, block), jnp.int32),
            pltpu.VMEM((1, block), jnp.int32),
            pltpu.VMEM((width_max, block), BF16),
            pltpu.VMEM((ntm, prow, block), BF16),
            pltpu.VMEM((nu, nu), BF16),
            pltpu.VMEM((share, nu), BF16),
            pltpu.VMEM((CORES * share, nu), BF16),
            pltpu.VMEM((ntm, half, nu), F32),
            pltpu.VMEM((ntm, half, nu), BF16),
            pltpu.VMEM((ntm - 1, half, nu - quarter), BF16),
            pltpu.VMEM((nz, own, nu - quarter), BF16),
            pltpu.VMEM((nz, own, nu - quarter), BF16),
            pltpu.VMEM((nz, ntm, own, quarter), BF16),
            pltpu.VMEM((ntm, own, quarter), F32),
            pltpu.VMEM((ntm, own, quarter), BF16),
            pltpu.VMEM((ntm - 1, own, quarter), BF16),
            pltpu.VMEM((CORES, ntm, half, nmode), BF16),
            pltpu.SemaphoreType.REGULAR((3,)),
            dma((5,)),
            dma((1,)),
            dma((1,)),
            dma((1,)),
            dma((chunks,)),
            dma((1,)),
            dma((chunks,)),
            dma((3,)),
            dma((3,)),
            dma((1,)),
            dma((2,)),
            dma((1,)),
            dma((2,)),
            dma((2,)),
            dma((2,)),
        ],
        compiler_params=pltpu.CompilerParams(
            collective_id=0, has_side_effects=True, vmem_limit_bytes=48 * 1024 * 1024
        ),
    )
    operands = (
        snapshots, stencil_starts.reshape(1, block), stencil_widths.reshape(1, block), stencil_coeffs.T, panels
    )
    values = call(*(pltpu.with_memory_space_constraint(operand, pltpu.HBM) for operand in operands))
    return pl.pallas_call(
        store,
        out_shape=tuple(jax.ShapeDtypeStruct(value.shape, value.dtype) for value in values),
        in_specs=[vmem, vmem],
        out_specs=(hbm, hbm),
        scratch_shapes=[dma((2,))],
    )(*(pltpu.with_memory_space_constraint(value, pltpu.VMEM) for value in values))


def store(gram, modes, gram_out, modes_out, sem):
    copies = [
        pltpu.make_async_copy(modes, modes_out, sem.at[0]),
        pltpu.make_async_copy(gram, gram_out, sem.at[1]),
    ]
    for copy in copies:
        copy.start()
    for copy in copies:
        copy.wait()


def solution(mesh):
    nsp, ntm = mesh.shape["space"], mesh.shape["tm"]

    def body(snapshots, stencil_starts, stencil_widths, stencil_coeffs, panels):
        rows, block = snapshots.shape
        own = block // nsp
        fits = block == 128 and own % 16 == 0 and nsp % (CORES * CORES) == 0 and 2 <= ntm <= 4 and ntm & (ntm - 1) == 0 and rows % (256 * ntm) == 0 and block * ntm % 512 == 0
        if fits and 4 * (block * ntm) ** 2 <= 4 * 1024 * 1024:
            return fused(nsp, ntm, snapshots, stencil_starts, stencil_widths, stencil_coeffs, panels)
        return on_device(snapshots, stencil_starts, stencil_widths, stencil_coeffs, panels)

    return jax.shard_map(
        body,
        mesh=mesh,
        in_specs=(P("space", "tm"), P("tm"), P("tm"), P("tm", None), P("tm", None)),
        out_specs=(P(("tm", "space"), None), P(("space", "tm"), None)),
        check_vma=False,
    )
```
